32 devices in a mesh: section: 4 (over x, core), expert: 8 (over z, y).
Axes of the slice: x: 2, y: 2, z: 4, core: 2. Of those that a mesh axis runs over, the one named last changes fastest.
Arguments:
- grad_rows: bfloat16 [4, 2, 1024, 1024], P('section', None, 'expert'), may hold values from -1 to 1
- owner_ids: int32 [4, 2, 1024, 1], P('section', None, 'expert'), may hold values from 0 to 7; in each aligned block of 128 rows (0 to 127, 128 to 255, ..., all dimensions but the last counted through in order) at most 32 rows name the same one
- saved_hidden: bfloat16 [4, 2, 8, 256, 384], P('section', None, 'expert'), may hold values from -6 to 6
- momentum: bfloat16 [4, 8, 384, 1024], P('section', 'expert'), may hold values from -32 to 32
Outputs:
- new_momentum: bfloat16 [4, 8, 384, 1024], P('section', 'expert')
- update_step: bfloat16 [4, 8, 384, 1024], P('section', 'expert')
The draws below stay inside these ranges and needn't reach their ends.
Inputs may be any that keep to these rules, and one draw needn't show every extreme that they name: `owner_ids`: within each aligned block of 128 rows of one section and direction, no owner is named by more than 32 rows, a bound that some block reaches.
All inputs are finite; a program needn't handle non-finite values.
Results may differ from the reference program's by a relative error of at most 0.0065.
Values may be sent and summed in bfloat16 or wider, within the bound.
No kernel may reach another device: no remote copies, remote signals or barrier semaphores. Data moves between devices by JAX's collectives and lax.ppermute only.
A program may use at most 64 MiB of HBM per device.

```python
import math
import jax
import jax.numpy as jnp
import numpy as np
from jax import lax

D = 1024
FF = 384
ROWS_DEV = 128
ITERS = 2
SECTIONS = 4
EXPERTS = 8
CAP = 32
SLOTS = 256
ROWS = 1024


def draw_momentum(key, part):
    key_rows = jax.random.fold_in(key, 11)
    key_cols = jax.random.fold_in(key, 12)
    key_base = jax.random.fold_in(key, 13)
    row_scale = jnp.exp(jax.random.uniform(key_rows, (SECTIONS, EXPERTS, FF, 1), jnp.float32, 0.0, 1.1513))
    col_scale = jnp.exp(jax.random.uniform(key_cols, (SECTIONS, EXPERTS, 1, D), jnp.float32, 0.0, 1.1513))
    values = jax.random.normal(key_base, (SECTIONS, EXPERTS, FF, D), jnp.float32)
    return jnp.clip(0.5 * row_scale * col_scale * values, -32.0, 32.0).astype(jnp.bfloat16)


def steps_of(key, dims, shards, smallest, high):
    def one(dim, parts):
        draws = jax.random.uniform(jax.random.fold_in(jax.random.fold_in(key, 6), dim), (parts,), jnp.float32, smallest / len(shards), high / len(shards))
        return jnp.repeat(jnp.exp(draws), dims[dim] // parts).reshape((-1,) + (1,) * (len(dims) - dim - 1))

    level = one(*shards[0])
    for cut in shards[1:]:
        level = level * one(*cut)
    return level


def routed_block(own_key, own, number, rows, count, top, bound, lean):
    ranking = jax.random.permutation(own_key, count)
    crowded, common = load_shares(count, rows * top, bound, lean, True), load_shares(count, rows * top, bound, lean, False)
    places = jnp.arange(count)

    def named(sizes, offset_by):
        used = int((sizes > 0).sum())
        fixed = max(1, used // 4)
        moved = fixed + (places - fixed + offset_by * (used - fixed)) % max(1, count - fixed)
        return jnp.zeros((count,), jnp.int32).at[ranking[jnp.where(places < fixed, places, moved)]].set(jnp.asarray(sizes, jnp.int32))

    sizes = jnp.where(number % 4 == 0, named(crowded, number // 4), named(common, number - number // 4 - 1))
    mixed = jax.random.permutation(jax.random.fold_in(own, 3), count)
    source_of, taker = mixed[0:count // 2 * 2:2], mixed[1:count // 2 * 2:2]
    room = jnp.minimum(sizes[source_of] - 1, bound - sizes[taker]) // 2
    room = jnp.where((source_of == ranking[0]) | (taker == ranking[0]) | (sizes[taker] == 0), 0, jnp.maximum(room, 0))
    moved = jax.random.randint(jax.random.fold_in(own, 4), (count // 2,), 0, 1 << 20) % (room + 1)
    sizes = sizes.at[source_of].add(-moved).at[taker].add(moved)
    labels = jnp.searchsorted(jnp.cumsum(sizes), jnp.arange(rows * top), side="right").astype(jnp.int32)
    grid = labels.reshape(top, rows).T
    grid = grid[jax.random.permutation(jax.random.fold_in(own, 1), rows)]
    offset_by = jax.random.randint(jax.random.fold_in(own, 2), (rows, 1), 0, top)
    return jnp.take_along_axis(grid, (jnp.arange(top)[None, :] + offset_by) % top, axis=1)


def load_shares(count, total, most, lean, full):
    loads = [(1 << 20) // math.isqrt(standing ** lean) + 1 for standing in range(1, count + 1)]
    largest = most if full else min(most, max(-(-total // count), total * loads[0] // sum(loads)))
    least = 1 if total - largest >= count - 1 else 0
    holding, spare = [largest] + [least] * (count - 1), total - largest - least * (count - 1)
    while spare > 0:
        candidates = [i for i in range(1, count) if holding[i] < largest] or [i for i in range(1, count) if holding[i] < most]
        whole, left = sum([loads[i] for i in candidates]), spare
        for i in candidates:
            addition = min(most - holding[i], max(1, left * loads[i] // whole), spare)
            holding[i] = holding[i] + addition
            spare = spare - addition
    return np.array(holding)


def bell_draw(rng, extent, deviation, reach, pieces=(), kind=jnp.bfloat16):
    result = jax.random.normal(rng, extent, jnp.float32) * deviation
    if len(pieces) > 0:
        result = steps_of(rng, extent, pieces, -0.22, 0.18) * result
    return jnp.clip(result, min=-reach, max=reach).astype(kind)


def setup_inputs(seed: int = 0) -> dict:
    seeds = jax.random.split(jax.random.key(seed), 5)
    grad_rows = bell_draw(seeds[0], (SECTIONS, 2, ROWS, D), 0.125, 1.0, ((0, 4), (2, 8)))
    owner_ids_keys = jax.random.split(jax.random.fold_in(seeds[1], 1), SECTIONS * 2 * ROWS // ROWS_DEV)
    owner_ids_turns = jax.random.permutation(jax.random.fold_in(seeds[1], 3), SECTIONS * 2 * ROWS // ROWS_DEV)
    owner_ids = jax.vmap(lambda own, number: routed_block(jax.random.fold_in(seeds[1], 2), own, number, ROWS_DEV, EXPERTS, 1, CAP, 2))(owner_ids_keys, owner_ids_turns).reshape((SECTIONS, 2, ROWS, 1))
    saved_hidden = bell_draw(seeds[2], (SECTIONS, 2, EXPERTS, SLOTS, FF), 1.0, 6.0, ((0, 4), (2, 8)))
    momentum = draw_momentum(jax.random.fold_in(seeds[4], 71), 0)
    return dict(grad_rows=grad_rows, owner_ids=owner_ids, saved_hidden=saved_hidden, momentum=momentum)


momentum_decay = 0.95
coef_first = 3.4445
coef_second = -4.775
coef_third = 2.0315
norm_epsilon = 1e-06

def slot_rows(row_block, owners):
    owner_grid = owners.reshape(EXPERTS, ROWS_DEV).astype(jnp.int32)
    onehot = (owner_grid[:, :, None] == jnp.arange(EXPERTS, dtype=jnp.int32)[None, None, :]).astype(jnp.int32)
    before = jnp.cumsum(onehot, axis=1) - onehot
    within = lax.optimization_barrier(jnp.sum(before * onehot, axis=2))
    source_index = jnp.arange(EXPERTS, dtype=jnp.int32)[:, None]
    target = owner_grid * SLOTS + source_index * CAP + within
    placed = jnp.zeros((EXPERTS * SLOTS, D), jnp.bfloat16).at[target.reshape(-1)].set(row_block)
    return placed.reshape(EXPERTS, SLOTS, D)

def contract(hidden_block, grad_block):
    product = lax.dot_general(hidden_block, grad_block, (((0,), (0,)), ((), ())), preferred_element_type=jnp.float32)
    return product.astype(jnp.bfloat16)

def orthogonalize(accum):
    norm_scale = jnp.sqrt(jnp.sum(accum * accum)) + norm_epsilon
    current = (accum / norm_scale).astype(jnp.bfloat16)
    for iteration in range(ITERS):
        gram_matrix = jnp.dot(current, current.T, preferred_element_type=jnp.float32).astype(jnp.bfloat16)
        once_applied = jnp.dot(gram_matrix, current, preferred_element_type=jnp.float32).astype(jnp.bfloat16)
        twice_applied = jnp.dot(gram_matrix, once_applied, preferred_element_type=jnp.float32).astype(jnp.bfloat16)
        combined = coef_first * current.astype(jnp.float32) + coef_second * once_applied.astype(jnp.float32) + coef_third * twice_applied.astype(jnp.float32)
        if iteration == ITERS - 1:
            combined = combined * math.sqrt(D)
        current = combined.astype(jnp.bfloat16)
    return current

def reference(grad_rows, owner_ids, saved_hidden, momentum):

    def one_layer(layer_index):
        mirror = SECTIONS - 1 - layer_index
        front_slots = slot_rows(grad_rows[layer_index, 0], owner_ids[layer_index, 0, :, 0])
        back_slots = slot_rows(grad_rows[mirror, 1], owner_ids[mirror, 1, :, 0])

        def one_expert(expert_index):
            near_part = contract(saved_hidden[layer_index, 0, expert_index], front_slots[expert_index])
            far_part = contract(saved_hidden[mirror, 1, expert_index], back_slots[expert_index])
            accum = momentum_decay * momentum[layer_index, expert_index].astype(jnp.float32) + near_part.astype(jnp.float32) + far_part.astype(jnp.float32)
            return (accum.astype(jnp.bfloat16), orthogonalize(accum))
        return lax.map(one_expert, jnp.arange(EXPERTS, dtype=jnp.int32))
    new_momentum, update_step = lax.map(one_layer, jnp.arange(SECTIONS, dtype=jnp.int32))
    return (new_momentum, update_step)
```

```python
import functools
import math

import jax
import jax.numpy as jnp
from jax import lax
from jax.experimental import pallas as pl
from jax.experimental.pallas import tpu as pltpu
from jax.sharding import PartitionSpec as P

ITERS = 2

momentum_decay = 0.95
coef_first = 3.4445
coef_second = -4.775
coef_third = 2.0315
norm_epsilon = 1e-06


def own_half(sections):
    section = lax.axis_index("section")
    return (section >= sections // 2).astype(jnp.int32)


def pack_kernel(peers, capacity, sections, ids_ref, rows_ref, out_ref):
    count = rows_ref.shape[1]
    slots = peers * capacity
    half = own_half(sections)
    earlier = (
        lax.broadcasted_iota(jnp.int32, (count, count), 0)
        < lax.broadcasted_iota(jnp.int32, (count, count), 1)
    ).astype(jnp.bfloat16)
    for direction in range(2):
        owners = ids_ref[direction]
        onehot = lax.broadcasted_iota(jnp.int32, (peers, count), 0) == owners
        before = jnp.dot(
            onehot.astype(jnp.bfloat16), earlier, preferred_element_type=jnp.float32
        )
        within = jnp.sum(jnp.where(onehot, before, 0.0), axis=0, keepdims=True)
        target = owners * capacity + within.astype(jnp.int32)
        place = lax.broadcasted_iota(jnp.int32, (slots, count), 0) == target
        packed = jnp.dot(
            place.astype(jnp.bfloat16), rows_ref[direction], preferred_element_type=jnp.float32
        ).astype(jnp.bfloat16)
        out_ref[half if direction == 0 else 1 - half] = packed


def pack(ids, rows, peers, capacity, sections):
    count, width = rows.shape[1:]
    return pl.pallas_call(
        functools.partial(pack_kernel, peers, capacity, sections),
        out_shape=jax.ShapeDtypeStruct((2, peers * capacity, width), jnp.bfloat16),
        in_specs=[pl.BlockSpec(memory_space=pltpu.VMEM)] * 2,
        out_specs=pl.BlockSpec(memory_space=pltpu.VMEM),
        name="pack",
    )(ids.reshape(2, 1, count), rows)


def contract(hidden_block, grad_block):
    return lax.dot_general(
        hidden_block, grad_block, (((0,), (0,)), ((), ())), preferred_element_type=jnp.float32
    ).astype(jnp.bfloat16).astype(jnp.float32)


def finish_kernel(
    sections, rows_ref, near_ref, far_ref, momentum_ref, new_ref, step_ref, current, sems
):
    height, width = momentum_ref.shape
    half = own_half(sections)
    chunk = min(256, width)
    columns = [pl.ds(start, chunk) for start in range(0, width, chunk)]
    squares = jnp.zeros((8, chunk), jnp.float32)
    for cols in columns:
        accum = momentum_decay * momentum_ref[:, cols].astype(jnp.float32)
        accum += contract(near_ref[...], rows_ref[half, :, cols])
        accum += contract(far_ref[...], rows_ref[1 - half, :, cols])
        current[:, cols] = accum
        squares += jnp.sum((accum * accum).reshape(height // 8, 8, chunk), axis=0)
        new_ref[:, cols] = accum.astype(jnp.bfloat16)
    inverse = 1.0 / (jnp.sqrt(jnp.sum(squares)) + norm_epsilon)
    for cols in columns:
        step_ref[:, cols] = (current[:, cols] * inverse).astype(jnp.bfloat16)
    for iteration in range(ITERS):
        whole = step_ref[...]
        gram = lax.dot_general(
            whole, whole, (((1,), (1,)), ((), ())), preferred_element_type=jnp.float32
        ).astype(jnp.bfloat16)
        square = jnp.dot(gram, gram, preferred_element_type=jnp.float32)
        factor = (coef_second * gram.astype(jnp.float32) + coef_third * square).astype(
            jnp.bfloat16
        )
        scale = math.sqrt(width) if iteration == ITERS - 1 else 1.0
        for cols in columns:
            block = step_ref[:, cols]
            applied = jnp.dot(factor, block, preferred_element_type=jnp.float32)
            combined = coef_first * block.astype(jnp.float32) + applied
            if iteration == ITERS - 1:
                combined = combined * scale
            step_ref[:, cols] = combined.astype(jnp.bfloat16)


def finish(rows, near, far, momentum, sections):
    shape = jax.ShapeDtypeStruct(momentum.shape, jnp.bfloat16)
    return pl.pallas_call(
        functools.partial(finish_kernel, sections),
        out_shape=(shape, shape),
        in_specs=[pl.BlockSpec(memory_space=pltpu.VMEM)] * 4,
        out_specs=[pl.BlockSpec(memory_space=pltpu.VMEM)] * 2,
        scratch_shapes=[
            pltpu.VMEM(momentum.shape, jnp.float32),
            pltpu.SemaphoreType.DMA((2,)),
        ],
        name="finish",
    )(*(pltpu.with_memory_space_constraint(x, pltpu.VMEM) for x in (rows, near, far, momentum)))


def per_device(grad_rows, owner_ids, saved_hidden, momentum):
    sections = lax.axis_size("section")
    peers = lax.axis_size("expert")
    slots = saved_hidden.shape[3]
    capacity = slots // peers
    width = grad_rows.shape[3]
    packed = pack(owner_ids[0], grad_rows[0], peers, capacity, sections)
    groups = [
        [section * peers + expert for section in (first, sections - 1 - first) for expert in range(peers)]
        for first in range(sections // 2)
    ]
    arrived = lax.all_to_all(
        packed.reshape(2 * peers, capacity, width),
        ("section", "expert"),
        split_axis=0,
        concat_axis=0,
        axis_index_groups=groups,
        tiled=True,
    ).reshape(2, slots, width)
    far_hidden = lax.ppermute(
        saved_hidden[0, 1, 0], "section", [(i, sections - 1 - i) for i in range(sections)]
    )
    new_momentum, update_step = finish(
        arrived, saved_hidden[0, 0, 0], far_hidden, momentum[0, 0], sections
    )
    return (new_momentum[None, None], update_step[None, None])


def solution(mesh):
    placed = (
        P("section", None, "expert", None),
        P("section", None, "expert", None),
        P("section", None, "expert", None, None),
        P("section", "expert", None, None),
    )
    return jax.shard_map(
        per_device,
        mesh=mesh,
        in_specs=placed,
        out_specs=(P("section", "expert", None, None), P("section", "expert", None, None)),
        check_vma=False,
    )
```

```python
import functools
import math

import jax
import jax.numpy as jnp
from jax import lax
from jax.experimental import pallas as pl
from jax.experimental.pallas import tpu as pltpu
from jax.sharding import PartitionSpec as P

ITERS = 2
TILE_ROWS = 16
PIECES = 1

momentum_decay = 0.95
coef_first = 3.4445
coef_second = -4.775
coef_third = 2.0315
norm_epsilon = 1e-06

VMEM = pl.BlockSpec(memory_space=pltpu.VMEM)
ANY = pl.BlockSpec(memory_space=pl.ANY)


def whole_call(body, out_shape, operands, scratch=(), in_spec=VMEM, out_spec=VMEM):
    return pl.pallas_call(
        body,
        out_shape=out_shape,
        in_specs=[in_spec] * len(operands),
        out_specs=out_spec if isinstance(out_spec, tuple) else (out_spec,) * len(out_shape) if isinstance(out_shape, tuple) else out_spec,
        scratch_shapes=list(scratch),
    )(*operands)


def in_vmem(array):
    return pltpu.with_memory_space_constraint(array, pltpu.VMEM)


def own_half(sections):
    return (lax.axis_index("section") >= sections // 2).astype(jnp.int32)


def placement(owners, slots, capacity):
    count = owners.shape[1]
    peers = slots // capacity
    earlier = (
        lax.broadcasted_iota(jnp.int32, (count, count), 0)
        < lax.broadcasted_iota(jnp.int32, (count, count), 1)
    ).astype(jnp.bfloat16)
    onehot = lax.broadcasted_iota(jnp.int32, (peers, count), 0) == owners
    before = jnp.dot(onehot.astype(jnp.bfloat16), earlier, preferred_element_type=jnp.float32)
    within = jnp.sum(jnp.where(onehot, before, 0.0), axis=0, keepdims=True)
    target = owners * capacity + within.astype(jnp.int32)
    return (lax.broadcasted_iota(jnp.int32, (slots, count), 0) == target).astype(jnp.bfloat16)


def place(matrix, rows):
    return jnp.dot(matrix, rows, preferred_element_type=jnp.float32).astype(jnp.bfloat16)


def pack_kernel(peers, capacity, sections, ids_ref, rows_ref, out_ref):
    half = own_half(sections)
    for direction in range(2):
        packed = place(placement(ids_ref[direction], peers * capacity, capacity), rows_ref[direction])
        out_ref[half if direction == 0 else 1 - half] = packed


def pack_split_kernel(peers, capacity, sections, ids_hbm, rows_hbm, hidden_hbm, joint_hbm, *refs):
    near_peers = peers // 2
    part = near_peers * capacity
    pairs = near_peers // 2
    *single_refs, near_out, far_out, ids, rows, hidden, joint, sems = refs
    count = rows.shape[1]
    step = count // PIECES
    ids_copy = pltpu.make_async_copy(ids_hbm, ids, sems.at[0, 0])
    ids_copy.start()
    row_copies = []
    for direction in range(2):
        for piece in range(PIECES):
            span = pl.ds(piece * step, step)
            copy = pltpu.make_async_copy(
                rows_hbm.at[direction, span], rows.at[direction, span], sems.at[1 + direction, piece]
            )
            copy.start()
            row_copies.append(copy)
    hidden_copies = [
        pltpu.make_async_copy(hidden_hbm.at[direction], hidden.at[direction], sems.at[4, direction])
        for direction in range(2)
    ]
    for copy in hidden_copies:
        copy.start()
    half = own_half(sections)
    me = lax.axis_index("expert")
    ids_copy.wait()
    matrices = []
    for direction in range(2):
        owners = ids[direction]
        distance = owners ^ me
        joint_xor = direction * near_peers
        inside = jnp.where((distance & near_peers) == joint_xor, owners & (near_peers - 1),
                           near_peers + (distance & (near_peers - 1)))
        matrices.append(placement(inside, peers * capacity, capacity))
    out_copies = []
    for direction in range(2):
        for copy in row_copies[direction * PIECES : (direction + 1) * PIECES]:
            copy.wait()
        joint[direction] = place(matrices[direction][:part], rows[direction])
        copy = pltpu.make_async_copy(
            joint.at[direction],
            joint_hbm.at[half if direction == 0 else 1 - half],
            sems.at[3, direction],
        )
        copy.start()
        out_copies.append(copy)
    for direction in range(2):
        packed = place(matrices[direction][part:], rows[direction])
        offset = 0
        for ref in single_refs[:pairs] if direction == 0 else single_refs[pairs:]:
            ref[...] = packed[offset : offset + ref.shape[0]]
            offset += ref.shape[0]
    own_part = me & near_peers
    for direction, out_ref in ((0, near_out), (1, far_out)):
        hidden_copies[direction].wait()
        first = own_part if direction == 0 else near_peers - own_part
        blocks = [hidden[direction, pl.ds(pl.multiple_of(first * capacity, part), part), :]]
        for index in range(near_peers):
            source = me ^ (index + near_peers if direction == 0 else index)
            start = pl.multiple_of(source * capacity, capacity)
            blocks.append(hidden[direction, pl.ds(start, capacity), :])
        out_ref[...] = jnp.concatenate(blocks, axis=0).T
    for copy in out_copies:
        copy.wait()


def contract(hidden_block, grad_block):
    return lax.dot_general(
        hidden_block, grad_block, (((0,), (0,)), ((), ())), preferred_element_type=jnp.float32
    ).astype(jnp.bfloat16).astype(jnp.float32)


def update(read_rows, near_ref, far_ref, momentum_ref, new_ref, step_ref, current):
    height, width = momentum_ref.shape
    chunk = min(256, width)
    columns = [pl.ds(start, chunk) for start in range(0, width, chunk)]
    squares = jnp.zeros((8, chunk), jnp.float32)
    for cols in columns:
        accum = momentum_decay * momentum_ref[:, cols].astype(jnp.float32)
        accum += contract(near_ref[...], read_rows(0, cols))
        accum += contract(far_ref[...], read_rows(1, cols))
        current[:, cols] = accum
        squares += jnp.sum((accum * accum).reshape(height // 8, 8, chunk), axis=0)
        new_ref[:, cols] = accum.astype(jnp.bfloat16)
    inverse = 1.0 / (jnp.sqrt(jnp.sum(squares)) + norm_epsilon)
    for cols in columns:
        step_ref[:, cols] = (current[:, cols] * inverse).astype(jnp.bfloat16)
    for iteration in range(ITERS):
        whole = step_ref[...]
        gram = lax.dot_general(
            whole, whole, (((1,), (1,)), ((), ())), preferred_element_type=jnp.float32
        ).astype(jnp.bfloat16)
        square = jnp.dot(gram, gram, preferred_element_type=jnp.float32)
        factor = (coef_second * gram.astype(jnp.float32) + coef_third * square).astype(
            jnp.bfloat16
        )
        for cols in columns:
            block = step_ref[:, cols]
            applied = jnp.dot(factor, block, preferred_element_type=jnp.float32)
            combined = coef_first * block.astype(jnp.float32) + applied
            if iteration == ITERS - 1:
                combined = combined * math.sqrt(width)
            step_ref[:, cols] = combined.astype(jnp.bfloat16)


def finish_kernel(sections, rows_ref, near_ref, far_ref, momentum_ref, new_ref, step_ref, current):
    half = own_half(sections)

    def read_rows(direction, cols):
        return rows_ref[half if direction == 0 else 1 - half, :, cols]

    update(read_rows, near_ref, far_ref, momentum_ref, new_ref, step_ref, current)


def finish_split_kernel(peers, sections, joint_ref, *refs):
    near_peers = peers // 2
    pairs = near_peers // 2
    pair_refs, relay_refs, single_refs = refs[:pairs], refs[pairs : 2 * pairs], refs[2 * pairs : 4 * pairs]
    near_ref, far_ref, momentum_ref, new_hbm, step_hbm, new_ref, step_ref, sems = refs[4 * pairs :]
    capacity = relay_refs[0].shape[0]
    half = own_half(sections)
    height, width = momentum_ref.shape
    chunk = min(256, width)
    columns = [pl.ds(start, chunk) for start in range(0, width, chunk)]

    def copies(ref, hbm, row):
        return [
            pltpu.make_async_copy(ref.at[:, cols], hbm.at[:, cols], sems.at[row, index])
            for index, cols in enumerate(columns)
        ]

    new_copies, step_copies = copies(new_ref, new_hbm, 0), copies(step_ref, step_hbm, 1)
    hidden = jnp.concatenate([near_ref[...], far_ref[...]], axis=1)
    for cols, copy in zip(columns, new_copies):
        rows = jnp.concatenate(
            [joint_ref[half, :, cols]]
            + [
                block
                for pair, relay in zip(pair_refs, relay_refs)
                for block in (pair[:capacity, cols], relay[:, cols])
            ]
            + [joint_ref[1 - half, :, cols]]
            + [ref[:, cols] for ref in single_refs],
            axis=0,
        )
        accum = jnp.dot(hidden, rows, preferred_element_type=jnp.float32)
        accum += momentum_decay * momentum_ref[:, cols].astype(jnp.float32)
        new_ref[:, cols] = accum.astype(jnp.bfloat16)
        copy.start()
    squares = jnp.zeros((8, chunk), jnp.float32)
    for cols in columns:
        block = new_ref[:, cols].astype(jnp.float32)
        squares += jnp.sum((block * block).reshape(height // 8, 8, chunk), axis=0)
    inverse = 1.0 / (jnp.sqrt(jnp.sum(squares)) + norm_epsilon)
    for iteration in range(ITERS):
        source_ref = new_ref if iteration == 0 else step_ref
        whole = source_ref[...]
        gram = lax.dot_general(whole, whole, (((1,), (1,)), ((), ())), preferred_element_type=jnp.float32)
        scale = coef_first
        if iteration == 0:
            gram = gram * (inverse * inverse)
            scale = scale * inverse
        if iteration == ITERS - 1:
            scale = scale * math.sqrt(width)
        gram = gram.astype(jnp.bfloat16)
        square = jnp.dot(gram, gram, preferred_element_type=jnp.float32)
        factor = (
            (coef_second / coef_first) * gram.astype(jnp.float32) + (coef_third / coef_first) * square
        ).astype(jnp.bfloat16)
        for cols, copy in zip(columns, step_copies):
            block = source_ref[:, cols]
            applied = jnp.dot(factor, block, preferred_element_type=jnp.float32)
            step_ref[:, cols] = (scale * (block.astype(jnp.float32) + applied)).astype(jnp.bfloat16)
            if iteration == ITERS - 1:
                copy.start()
    for copy in new_copies + step_copies:
        copy.wait()


def joint_groups(sections, peers, split):
    mirror = lambda section: sections - 1 - section
    if not split:
        return [
            [section * peers + expert for section in (first, mirror(first)) for expert in range(peers)]
            for first in range(sections // 2)
        ]
    count = peers // 2
    return [
        [first * peers + part * count + index for index in range(count)]
        + [mirror(first) * peers + (1 - part) * count + index for index in range(count)]
        for first in range(sections // 2)
        for part in range(2)
    ]


def direct(block, sections, peers, distance, crossing):
    pairs = [
        (
            section * peers + expert,
            (sections - 1 - section if crossing else section) * peers + (expert ^ distance),
        )
        for section in range(sections)
        for expert in range(peers)
    ]
    return lax.ppermute(block, ("section", "expert"), pairs)


def exchange(blocks, groups):
    return lax.all_to_all(
        blocks, ("section", "expert"), split_axis=0, concat_axis=0, axis_index_groups=groups, tiled=True
    )


def splits(peers, capacity):
    return peers > 2 and peers & (peers - 1) == 0 and capacity % TILE_ROWS == 0


def per_device(grad_rows, owner_ids, saved_hidden, momentum):
    sections = lax.axis_size("section")
    peers = lax.axis_size("expert")
    slots = saved_hidden.shape[3]
    capacity = slots // peers
    count, width = grad_rows.shape[2:]
    ids = owner_ids[0].reshape(2, 1, count)
    shaped = lambda *shape: jax.ShapeDtypeStruct(shape, jnp.bfloat16)
    landing = lambda *shape: pltpu.VMEM(shape, jnp.bfloat16)
    last = (saved_hidden[0, 0, 0], momentum[0, 0])
    outs = (shaped(*momentum.shape[2:]),) * 2
    current = pltpu.VMEM(momentum.shape[2:], jnp.float32)
    split = splits(peers, capacity)
    groups = joint_groups(sections, peers, split)

    def hidden_over(hidden):
        return lax.ppermute(hidden, "section", [(i, sections - 1 - i) for i in range(sections)])

    if not split:
        packed = whole_call(
            functools.partial(pack_kernel, peers, capacity, sections),
            shaped(2, slots, width), (ids, grad_rows[0]),
        )
        arrived = exchange(packed.reshape(2 * peers, capacity, width), groups).reshape(2, slots, width)
        operands = (arrived, last[0], hidden_over(saved_hidden[0, 1, 0]), last[1])
        body = functools.partial(finish_kernel, sections)
        scratch = (current,)
    else:
        near_peers = peers // 2
        height = saved_hidden.shape[4]
        joint, *singles, near_hidden, turned = whole_call(
            functools.partial(pack_split_kernel, peers, capacity, sections),
            (shaped(2, near_peers * capacity, width),) + (landing(2 * capacity, width),) * (near_peers // 2)
            + (landing(capacity, width),) * near_peers
            + (landing(height, slots),) * 2,
            (ids, grad_rows[0], saved_hidden.reshape(2, slots, height)),
            (
                pltpu.VMEM(ids.shape, jnp.int32),
                pltpu.VMEM(grad_rows.shape[1:], jnp.bfloat16),
                pltpu.VMEM((2, slots, height), jnp.bfloat16),
                pltpu.VMEM((2, near_peers * capacity, width), jnp.bfloat16),
                pltpu.SemaphoreType.DMA((5, 2)),
            ),
            in_spec=ANY,
            out_spec=(ANY,) + (VMEM,) * (near_peers // 2 + near_peers + 2),
        )
        pairs = near_peers // 2
        landed, relayed, mirrored = [], [], []
        for index, block in enumerate(singles[:pairs]):
            landed.append(direct(block, sections, peers, near_peers + 2 * index, False))
        for index, block in enumerate(singles[pairs:]):
            mirrored.append(direct(block, sections, peers, index, True))
        for block in landed:
            relayed.append(direct(block[capacity:], sections, peers, 1, False))
        far_hidden = hidden_over(turned)
        arrived = exchange(joint.reshape(peers, capacity, width), groups)
        operands = (arrived.reshape(joint.shape), *landed, *relayed, *mirrored, near_hidden, far_hidden, last[1])
        body = functools.partial(finish_split_kernel, peers, sections)
        scratch = (
            pltpu.VMEM(momentum.shape[2:], jnp.bfloat16),
            pltpu.VMEM(momentum.shape[2:], jnp.bfloat16),
            pltpu.SemaphoreType.DMA((2, pl.cdiv(width, 256))),
        )
    new_momentum, update_step = whole_call(
        body, outs, tuple(map(in_vmem, operands)), scratch,
        out_spec=ANY if split else VMEM,
    )
    return (new_momentum[None, None], update_step[None, None])


def solution(mesh):
    placed = (
        P("section", None, "expert", None),
        P("section", None, "expert", None),
        P("section", None, "expert", None, None),
        P("section", "expert", None, None),
    )

    return jax.shard_map(
        per_device,
        mesh=mesh,
        in_specs=placed,
        out_specs=(P("section", "expert", None, None), P("section", "expert", None, None)),
        check_vma=False,
    )
```

```python
import functools
import math

import jax
import jax.numpy as jnp
from jax import lax
from jax.experimental import pallas as pl
from jax.experimental.pallas import tpu as pltpu
from jax.sharding import PartitionSpec as P

ITERS = 2
TILE_ROWS = 16
PIECES = 1

momentum_decay = 0.95
coef_first = 3.4445
coef_second = -4.775
coef_third = 2.0315
norm_epsilon = 1e-06

VMEM = pl.BlockSpec(memory_space=pltpu.VMEM)
ANY = pl.BlockSpec(memory_space=pl.ANY)


def whole_call(body, out_shape, operands, scratch=(), in_spec=VMEM, out_spec=VMEM):
    return pl.pallas_call(
        body,
        out_shape=out_shape,
        in_specs=[in_spec] * len(operands),
        out_specs=out_spec if isinstance(out_spec, tuple) else (out_spec,) * len(out_shape) if isinstance(out_shape, tuple) else out_spec,
        scratch_shapes=list(scratch),
    )(*operands)


def in_vmem(array):
    return pltpu.with_memory_space_constraint(array, pltpu.VMEM)


def own_half(sections):
    return (lax.axis_index("section") >= sections // 2).astype(jnp.int32)


def placement(owners, slots, capacity):
    count = owners.shape[1]
    peers = slots // capacity
    earlier = (
        lax.broadcasted_iota(jnp.int32, (count, count), 0)
        < lax.broadcasted_iota(jnp.int32, (count, count), 1)
    ).astype(jnp.bfloat16)
    onehot = lax.broadcasted_iota(jnp.int32, (peers, count), 0) == owners
    before = jnp.dot(onehot.astype(jnp.bfloat16), earlier, preferred_element_type=jnp.float32)
    within = jnp.sum(jnp.where(onehot, before, 0.0), axis=0, keepdims=True)
    target = owners * capacity + within.astype(jnp.int32)
    return (lax.broadcasted_iota(jnp.int32, (slots, count), 0) == target).astype(jnp.bfloat16)


def place(matrix, rows):
    return jnp.dot(matrix, rows, preferred_element_type=jnp.float32).astype(jnp.bfloat16)


def pack_kernel(peers, capacity, sections, ids_ref, rows_ref, out_ref):
    half = own_half(sections)
    for direction in range(2):
        packed = place(placement(ids_ref[direction], peers * capacity, capacity), rows_ref[direction])
        out_ref[half if direction == 0 else 1 - half] = packed


def pack_split_kernel(peers, capacity, sections, ids_hbm, rows_hbm, hidden_hbm, joint_hbm, *refs):
    near_peers = peers // 2
    part = near_peers * capacity
    pairs = near_peers // 2
    *single_refs, near_out, far_out, ids, rows, hidden, joint, sems = refs
    count = rows.shape[1]
    step = count // PIECES
    ids_copy = pltpu.make_async_copy(ids_hbm, ids, sems.at[0, 0])
    ids_copy.start()
    row_copies = []
    for direction in range(2):
        for piece in range(PIECES):
            span = pl.ds(piece * step, step)
            copy = pltpu.make_async_copy(
                rows_hbm.at[direction, span], rows.at[direction, span], sems.at[1 + direction, piece]
            )
            copy.start()
            row_copies.append(copy)
    hidden_copies = [
        pltpu.make_async_copy(hidden_hbm.at[direction], hidden.at[direction], sems.at[4, direction])
        for direction in range(2)
    ]
    for copy in hidden_copies:
        copy.start()
    half = own_half(sections)
    me = lax.axis_index("expert")
    ids_copy.wait()
    matrices = []
    for direction in range(2):
        owners = ids[direction]
        distance = owners ^ me
        joint_xor = direction * near_peers
        inside = jnp.where((distance & near_peers) == joint_xor, owners & (near_peers - 1),
                           near_peers + (distance & (near_peers - 1)))
        matrices.append(placement(inside, peers * capacity, capacity))
    out_copies = []
    for direction in range(2):
        for copy in row_copies[direction * PIECES : (direction + 1) * PIECES]:
            copy.wait()
        joint[direction] = place(matrices[direction][:part], rows[direction])
        copy = pltpu.make_async_copy(
            joint.at[direction],
            joint_hbm.at[half if direction == 0 else 1 - half],
            sems.at[3, direction],
        )
        copy.start()
        out_copies.append(copy)
    for direction in range(2):
        packed = place(matrices[direction][part:], rows[direction])
        offset = 0
        for ref in single_refs[:pairs] if direction == 0 else single_refs[pairs:]:
            ref[...] = packed[offset : offset + ref.shape[0]]
            offset += ref.shape[0]
    own_part = me & near_peers
    for direction, out_ref in ((0, near_out), (1, far_out)):
        hidden_copies[direction].wait()
        first = own_part if direction == 0 else near_peers - own_part
        blocks = [hidden[direction, pl.ds(pl.multiple_of(first * capacity, part), part), :]]
        for index in range(near_peers):
            source = me ^ (index + near_peers if direction == 0 else index)
            start = pl.multiple_of(source * capacity, capacity)
            blocks.append(hidden[direction, pl.ds(start, capacity), :])
        out_ref[...] = jnp.concatenate(blocks, axis=0).T
    for copy in out_copies:
        copy.wait()


def contract(hidden_block, grad_block):
    return lax.dot_general(
        hidden_block, grad_block, (((0,), (0,)), ((), ())), preferred_element_type=jnp.float32
    ).astype(jnp.bfloat16).astype(jnp.float32)


def update(read_rows, near_ref, far_ref, momentum_ref, new_ref, step_ref, current):
    height, width = momentum_ref.shape
    chunk = min(256, width)
    columns = [pl.ds(start, chunk) for start in range(0, width, chunk)]
    squares = jnp.zeros((8, chunk), jnp.float32)
    for cols in columns:
        accum = momentum_decay * momentum_ref[:, cols].astype(jnp.float32)
        accum += contract(near_ref[...], read_rows(0, cols))
        accum += contract(far_ref[...], read_rows(1, cols))
        current[:, cols] = accum
        squares += jnp.sum((accum * accum).reshape(height // 8, 8, chunk), axis=0)
        new_ref[:, cols] = accum.astype(jnp.bfloat16)
    inverse = 1.0 / (jnp.sqrt(jnp.sum(squares)) + norm_epsilon)
    for cols in columns:
        step_ref[:, cols] = (current[:, cols] * inverse).astype(jnp.bfloat16)
    for iteration in range(ITERS):
        whole = step_ref[...]
        gram = lax.dot_general(
            whole, whole, (((1,), (1,)), ((), ())), preferred_element_type=jnp.float32
        ).astype(jnp.bfloat16)
        square = jnp.dot(gram, gram, preferred_element_type=jnp.float32)
        factor = (coef_second * gram.astype(jnp.float32) + coef_third * square).astype(
            jnp.bfloat16
        )
        for cols in columns:
            block = step_ref[:, cols]
            applied = jnp.dot(factor, block, preferred_element_type=jnp.float32)
            combined = coef_first * block.astype(jnp.float32) + applied
            if iteration == ITERS - 1:
                combined = combined * math.sqrt(width)
            step_ref[:, cols] = combined.astype(jnp.bfloat16)


def finish_kernel(sections, rows_ref, near_ref, far_ref, momentum_ref, new_ref, step_ref, current):
    half = own_half(sections)

    def read_rows(direction, cols):
        return rows_ref[half if direction == 0 else 1 - half, :, cols]

    update(read_rows, near_ref, far_ref, momentum_ref, new_ref, step_ref, current)


def finish_split_kernel(peers, sections, joint_ref, *refs):
    near_peers = peers // 2
    pairs = near_peers // 2
    pair_refs, relay_refs, single_refs = refs[:pairs], refs[pairs : 2 * pairs], refs[2 * pairs : 4 * pairs]
    near_ref, far_ref, momentum_ref, new_hbm, step_hbm, new_ref, step_ref, sems = refs[4 * pairs :]
    capacity = relay_refs[0].shape[0]
    half = own_half(sections)
    height, width = momentum_ref.shape
    chunk = min(256, width)
    columns = [pl.ds(start, chunk) for start in range(0, width, chunk)]

    def copies(ref, hbm, row):
        return [
            pltpu.make_async_copy(ref.at[:, cols], hbm.at[:, cols], sems.at[row, index])
            for index, cols in enumerate(columns)
        ]

    new_copies, step_copies = copies(new_ref, new_hbm, 0), copies(step_ref, step_hbm, 1)
    hidden = jnp.concatenate([near_ref[...], far_ref[...]], axis=1)
    for cols, copy in zip(columns, new_copies):
        rows = jnp.concatenate(
            [joint_ref[half, :, cols]]
            + [
                block
                for pair, relay in zip(pair_refs, relay_refs)
                for block in (pair[:capacity, cols], relay[:, cols])
            ]
            + [joint_ref[1 - half, :, cols]]
            + [ref[:capacity, cols] for ref in single_refs],
            axis=0,
        )
        accum = jnp.dot(hidden, rows, preferred_element_type=jnp.float32)
        accum += momentum_decay * momentum_ref[:, cols].astype(jnp.float32)
        new_ref[:, cols] = accum.astype(jnp.bfloat16)
        copy.start()
    squares = jnp.zeros((8, chunk), jnp.float32)
    for cols in columns:
        block = new_ref[:, cols].astype(jnp.float32)
        squares += jnp.sum((block * block).reshape(height // 8, 8, chunk), axis=0)
    inverse = 1.0 / (jnp.sqrt(jnp.sum(squares)) + norm_epsilon)
    for iteration in range(ITERS):
        source_ref = new_ref if iteration == 0 else step_ref
        whole = source_ref[...]
        gram = lax.dot_general(whole, whole, (((1,), (1,)), ((), ())), preferred_element_type=jnp.float32)
        scale = coef_first
        if iteration == 0:
            gram = gram * (inverse * inverse)
            scale = scale * inverse
        if iteration == ITERS - 1:
            scale = scale * math.sqrt(width)
        gram = gram.astype(jnp.bfloat16)
        square = jnp.dot(gram, gram, preferred_element_type=jnp.float32)
        factor = (
            (coef_second / coef_first) * gram.astype(jnp.float32) + (coef_third / coef_first) * square
        ).astype(jnp.bfloat16)
        for cols, copy in zip(columns, step_copies):
            block = source_ref[:, cols]
            applied = jnp.dot(factor, block, preferred_element_type=jnp.float32)
            step_ref[:, cols] = (scale * (block.astype(jnp.float32) + applied)).astype(jnp.bfloat16)
            if iteration == ITERS - 1:
                copy.start()
    for copy in new_copies + step_copies:
        copy.wait()


def joint_groups(sections, peers, split):
    mirror = lambda section: sections - 1 - section
    if not split:
        return [
            [section * peers + expert for section in (first, mirror(first)) for expert in range(peers)]
            for first in range(sections // 2)
        ]
    count = peers // 2
    return [
        [first * peers + part * count + index for index in range(count)]
        + [mirror(first) * peers + (1 - part) * count + index for index in range(count)]
        for first in range(sections // 2)
        for part in range(2)
    ]


def direct(block, sections, peers, distance, crossing):
    pairs = [
        (
            section * peers + expert,
            (sections - 1 - section if crossing else section) * peers + (expert ^ distance),
        )
        for section in range(sections)
        for expert in range(peers)
    ]
    return lax.ppermute(block, ("section", "expert"), pairs)


def exchange(blocks, groups):
    return lax.all_to_all(
        blocks, ("section", "expert"), split_axis=0, concat_axis=0, axis_index_groups=groups, tiled=True
    )


def near_bundles(near_peers):
    return [(distance, 2) for distance in range(0, near_peers, 2)]


def splits(peers, capacity):
    return peers > 2 and peers & (peers - 1) == 0 and capacity % TILE_ROWS == 0


def per_device(grad_rows, owner_ids, saved_hidden, momentum):
    sections = lax.axis_size("section")
    peers = lax.axis_size("expert")
    slots = saved_hidden.shape[3]
    capacity = slots // peers
    count, width = grad_rows.shape[2:]
    ids = owner_ids[0].reshape(2, 1, count)
    shaped = lambda *shape: jax.ShapeDtypeStruct(shape, jnp.bfloat16)
    landing = lambda *shape: pltpu.VMEM(shape, jnp.bfloat16)
    last = (saved_hidden[0, 0, 0], momentum[0, 0])
    outs = (shaped(*momentum.shape[2:]),) * 2
    current = pltpu.VMEM(momentum.shape[2:], jnp.float32)
    split = splits(peers, capacity)
    groups = joint_groups(sections, peers, split)

    def hidden_over(hidden):
        return lax.ppermute(hidden, "section", [(i, sections - 1 - i) for i in range(sections)])

    if not split:
        packed = whole_call(
            functools.partial(pack_kernel, peers, capacity, sections),
            shaped(2, slots, width), (ids, grad_rows[0]),
        )
        arrived = exchange(packed.reshape(2 * peers, capacity, width), groups).reshape(2, slots, width)
        operands = (arrived, last[0], hidden_over(saved_hidden[0, 1, 0]), last[1])
        body = functools.partial(finish_kernel, sections)
        scratch = (current,)
    else:
        near_peers = peers // 2
        height = saved_hidden.shape[4]
        joint, *singles, near_hidden, turned = whole_call(
            functools.partial(pack_split_kernel, peers, capacity, sections),
            (shaped(2, near_peers * capacity, width),) + (landing(2 * capacity, width),) * (near_peers // 2)
            + tuple(landing(size * capacity, width) for _, size in near_bundles(near_peers))
            + (landing(height, slots),) * 2,
            (ids, grad_rows[0], saved_hidden.reshape(2, slots, height)),
            (
                pltpu.VMEM(ids.shape, jnp.int32),
                pltpu.VMEM(grad_rows.shape[1:], jnp.bfloat16),
                pltpu.VMEM((2, slots, height), jnp.bfloat16),
                pltpu.VMEM((2, near_peers * capacity, width), jnp.bfloat16),
                pltpu.SemaphoreType.DMA((5, 2)),
            ),
            in_spec=ANY,
            out_spec=(ANY,) + (VMEM,) * (near_peers // 2 + len(near_bundles(near_peers)) + 2),
        )
        pairs = near_peers // 2
        landed, relayed, mirrored = [], [], []
        for index, block in enumerate(singles[:pairs]):
            landed.append(direct(block, sections, peers, near_peers + 2 * index, False))
        for (distance, size), block in zip(near_bundles(near_peers), singles[pairs:]):
            block = direct(block, sections, peers, distance, True)
            mirrored.append(block)
            if size == 2:
                mirrored.append(direct(block[capacity:], sections, peers, 1, False))
        for block in landed:
            relayed.append(direct(block[capacity:], sections, peers, 1, False))
        far_hidden = hidden_over(turned)
        arrived = exchange(joint.reshape(peers, capacity, width), groups)
        operands = (arrived.reshape(joint.shape), *landed, *relayed, *mirrored, near_hidden, far_hidden, last[1])
        body = functools.partial(finish_split_kernel, peers, sections)
        scratch = (
            pltpu.VMEM(momentum.shape[2:], jnp.bfloat16),
            pltpu.VMEM(momentum.shape[2:], jnp.bfloat16),
            pltpu.SemaphoreType.DMA((2, pl.cdiv(width, 256))),
        )
    new_momentum, update_step = whole_call(
        body, outs, tuple(map(in_vmem, operands)), scratch,
        out_spec=ANY if split else VMEM,
    )
    return (new_momentum[None, None], update_step[None, None])


def solution(mesh):
    placed = (
        P("section", None, "expert", None),
        P("section", None, "expert", None),
        P("section", None, "expert", None, None),
        P("section", "expert", None, None),
    )

    return jax.shard_map(
        per_device,
        mesh=mesh,
        in_specs=placed,
        out_specs=(P("section", "expert", None, None), P("section", "expert", None, None)),
        check_vma=False,
    )
```

```python
import functools
import math

import jax
import jax.numpy as jnp
from jax import lax
from jax.experimental import pallas as pl
from jax.experimental.pallas import tpu as pltpu
from jax.sharding import PartitionSpec as P

ITERS = 2
TILE_ROWS = 16
PIECES = 1
WIDE, NARROW = 512, 256

momentum_decay = 0.95
coef_first = 3.4445
coef_second = -4.775
coef_third = 2.0315
norm_epsilon = 1e-06

VMEM = pl.BlockSpec(memory_space=pltpu.VMEM)
ANY = pl.BlockSpec(memory_space=pl.ANY)


def whole_call(body, out_shape, operands, scratch=(), in_spec=VMEM, out_spec=VMEM):
    return pl.pallas_call(
        body,
        out_shape=out_shape,
        in_specs=[in_spec] * len(operands),
        out_specs=out_spec if isinstance(out_spec, tuple) else (out_spec,) * len(out_shape) if isinstance(out_shape, tuple) else out_spec,
        scratch_shapes=list(scratch),
    )(*operands)


def in_vmem(array):
    return pltpu.with_memory_space_constraint(array, pltpu.VMEM)


def own_half(sections):
    return (lax.axis_index("section") >= sections // 2).astype(jnp.int32)


def placement(owners, slots, capacity):
    count = owners.shape[1]
    peers = slots // capacity
    earlier = (
        lax.broadcasted_iota(jnp.int32, (count, count), 0)
        < lax.broadcasted_iota(jnp.int32, (count, count), 1)
    ).astype(jnp.bfloat16)
    onehot = lax.broadcasted_iota(jnp.int32, (peers, count), 0) == owners
    before = jnp.dot(onehot.astype(jnp.bfloat16), earlier, preferred_element_type=jnp.float32)
    within = jnp.sum(jnp.where(onehot, before, 0.0), axis=0, keepdims=True)
    target = owners * capacity + within.astype(jnp.int32)
    return (lax.broadcasted_iota(jnp.int32, (slots, count), 0) == target).astype(jnp.bfloat16)


def place(matrix, rows):
    return jnp.dot(matrix, rows, preferred_element_type=jnp.float32).astype(jnp.bfloat16)


def pack_kernel(peers, capacity, sections, ids_ref, rows_ref, out_ref):
    half = own_half(sections)
    for direction in range(2):
        packed = place(placement(ids_ref[direction], peers * capacity, capacity), rows_ref[direction])
        out_ref[half if direction == 0 else 1 - half] = packed


def pack_split_kernel(peers, capacity, sections, ids_hbm, rows_hbm, hidden_hbm, joint_hbm, *refs):
    near_peers = peers // 2
    part = near_peers * capacity
    pairs = near_peers // 2
    *single_refs, near_out, far_out, ids, rows, hidden, joint, sems = refs
    count = rows.shape[1]
    step = count // PIECES
    ids_copy = pltpu.make_async_copy(ids_hbm, ids, sems.at[0, 0])
    ids_copy.start()
    row_copies = []
    for direction in range(2):
        for piece in range(PIECES):
            span = pl.ds(piece * step, step)
            copy = pltpu.make_async_copy(
                rows_hbm.at[direction, span], rows.at[direction, span], sems.at[1 + direction, piece]
            )
            copy.start()
            row_copies.append(copy)
    hidden_copies = [
        pltpu.make_async_copy(hidden_hbm.at[direction], hidden.at[direction], sems.at[4, direction])
        for direction in range(2)
    ]
    for copy in hidden_copies:
        copy.start()
    half = own_half(sections)
    me = lax.axis_index("expert")
    ids_copy.wait()
    matrices = []
    for direction in range(2):
        owners = ids[direction]
        distance = owners ^ me
        joint_xor = direction * near_peers
        inside = jnp.where((distance & near_peers) == joint_xor, owners & (near_peers - 1),
                           near_peers + (distance & (near_peers - 1)))
        matrices.append(placement(inside, peers * capacity, capacity))
    out_copies = []
    for direction in range(2):
        for copy in row_copies[direction * PIECES : (direction + 1) * PIECES]:
            copy.wait()
        joint[direction] = place(matrices[direction][:part], rows[direction])
        copy = pltpu.make_async_copy(
            joint.at[direction],
            joint_hbm.at[half if direction == 0 else 1 - half],
            sems.at[3, direction],
        )
        copy.start()
        out_copies.append(copy)
    for direction in range(2):
        packed = place(matrices[direction][part:], rows[direction])
        offset = 0
        for ref in single_refs[:pairs] if direction == 0 else single_refs[pairs:]:
            ref[...] = packed[offset : offset + ref.shape[0]]
            offset += ref.shape[0]
    own_part = me & near_peers
    for direction, out_ref in ((0, near_out), (1, far_out)):
        hidden_copies[direction].wait()
        first = own_part if direction == 0 else near_peers - own_part
        blocks = [hidden[direction, pl.ds(pl.multiple_of(first * capacity, part), part), :]]
        for index in range(near_peers):
            source = me ^ (index + near_peers if direction == 0 else index)
            start = pl.multiple_of(source * capacity, capacity)
            blocks.append(hidden[direction, pl.ds(start, capacity), :])
        out_ref[...] = jnp.concatenate(blocks, axis=0).T
    for copy in out_copies:
        copy.wait()


def contract(hidden_block, grad_block):
    return lax.dot_general(
        hidden_block, grad_block, (((0,), (0,)), ((), ())), preferred_element_type=jnp.float32
    ).astype(jnp.bfloat16).astype(jnp.float32)


def update(read_rows, near_ref, far_ref, momentum_ref, new_ref, step_ref, current):
    height, width = momentum_ref.shape
    chunk = min(256, width)
    columns = [pl.ds(start, chunk) for start in range(0, width, chunk)]
    squares = jnp.zeros((8, chunk), jnp.float32)
    for cols in columns:
        accum = momentum_decay * momentum_ref[:, cols].astype(jnp.float32)
        accum += contract(near_ref[...], read_rows(0, cols))
        accum += contract(far_ref[...], read_rows(1, cols))
        current[:, cols] = accum
        squares += jnp.sum((accum * accum).reshape(height // 8, 8, chunk), axis=0)
        new_ref[:, cols] = accum.astype(jnp.bfloat16)
    inverse = 1.0 / (jnp.sqrt(jnp.sum(squares)) + norm_epsilon)
    for cols in columns:
        step_ref[:, cols] = (current[:, cols] * inverse).astype(jnp.bfloat16)
    for iteration in range(ITERS):
        whole = step_ref[...]
        gram = lax.dot_general(
            whole, whole, (((1,), (1,)), ((), ())), preferred_element_type=jnp.float32
        ).astype(jnp.bfloat16)
        square = jnp.dot(gram, gram, preferred_element_type=jnp.float32)
        factor = (coef_second * gram.astype(jnp.float32) + coef_third * square).astype(
            jnp.bfloat16
        )
        for cols in columns:
            block = step_ref[:, cols]
            applied = jnp.dot(factor, block, preferred_element_type=jnp.float32)
            combined = coef_first * block.astype(jnp.float32) + applied
            if iteration == ITERS - 1:
                combined = combined * math.sqrt(width)
            step_ref[:, cols] = combined.astype(jnp.bfloat16)


def finish_kernel(sections, rows_ref, near_ref, far_ref, momentum_ref, new_ref, step_ref, current):
    half = own_half(sections)

    def read_rows(direction, cols):
        return rows_ref[half if direction == 0 else 1 - half, :, cols]

    update(read_rows, near_ref, far_ref, momentum_ref, new_ref, step_ref, current)


def finish_split_kernel(peers, sections, joint_ref, *refs):
    near_peers = peers // 2
    pairs = near_peers // 2
    pair_refs, relay_refs, single_refs = refs[:pairs], refs[pairs : 2 * pairs], refs[2 * pairs : 4 * pairs]
    near_ref, far_ref, momentum_ref, new_hbm, step_hbm, new_ref, step_ref, sems = refs[4 * pairs :]
    capacity = relay_refs[0].shape[0]
    half = own_half(sections)
    height, width = momentum_ref.shape
    chunk = min(WIDE, width)
    spans = lambda size: [pl.ds(start, size) for start in range(0, width, size)]
    columns, narrow = spans(chunk), spans(min(NARROW, width))

    def copies(ref, hbm, row, columns):
        return [
            pltpu.make_async_copy(ref.at[:, cols], hbm.at[:, cols], sems.at[row, index])
            for index, cols in enumerate(columns)
        ]

    new_copies, step_copies = copies(new_ref, new_hbm, 0, columns), copies(step_ref, step_hbm, 1, narrow)
    hidden = jnp.concatenate([near_ref[...], far_ref[...]], axis=1)
    for cols, copy in zip(columns, new_copies):
        rows = jnp.concatenate(
            [joint_ref[half, :, cols]]
            + [
                block
                for pair, relay in zip(pair_refs, relay_refs)
                for block in (pair[:capacity, cols], relay[:, cols])
            ]
            + [joint_ref[1 - half, :, cols]]
            + [ref[:capacity, cols] for ref in single_refs],
            axis=0,
        )
        accum = jnp.dot(hidden, rows, preferred_element_type=jnp.float32)
        accum += momentum_decay * momentum_ref[:, cols].astype(jnp.float32)
        new_ref[:, cols] = accum.astype(jnp.bfloat16)
        copy.start()
    squares = jnp.zeros((8, chunk), jnp.float32)
    for cols in columns:
        block = new_ref[:, cols].astype(jnp.float32)
        squares += jnp.sum((block * block).reshape(height // 8, 8, chunk), axis=0)
    inverse = 1.0 / (jnp.sqrt(jnp.sum(squares)) + norm_epsilon)
    for iteration in range(ITERS):
        source_ref = new_ref if iteration == 0 else step_ref
        whole = source_ref[...]
        gram = lax.dot_general(whole, whole, (((1,), (1,)), ((), ())), preferred_element_type=jnp.float32)
        scale = coef_first
        if iteration == 0:
            gram = gram * (inverse * inverse)
            scale = scale * inverse
        if iteration == ITERS - 1:
            scale = scale * math.sqrt(width)
        gram = gram.astype(jnp.bfloat16)
        square = jnp.dot(gram, gram, preferred_element_type=jnp.float32)
        factor = (
            (coef_second / coef_first) * gram.astype(jnp.float32) + (coef_third / coef_first) * square
        ).astype(jnp.bfloat16)
        final = iteration == ITERS - 1
        for index, cols in enumerate(narrow if final else columns):
            block = source_ref[:, cols]
            applied = jnp.dot(factor, block, preferred_element_type=jnp.float32)
            step_ref[:, cols] = (scale * (block.astype(jnp.float32) + applied)).astype(jnp.bfloat16)
            if final:
                step_copies[index].start()
    for copy in new_copies + step_copies:
        copy.wait()


def joint_groups(sections, peers, split):
    mirror = lambda section: sections - 1 - section
    if not split:
        return [
            [section * peers + expert for section in (first, mirror(first)) for expert in range(peers)]
            for first in range(sections // 2)
        ]
    count = peers // 2
    return [
        [first * peers + part * count + index for index in range(count)]
        + [mirror(first) * peers + (1 - part) * count + index for index in range(count)]
        for first in range(sections // 2)
        for part in range(2)
    ]


def direct(block, sections, peers, distance, crossing):
    pairs = [
        (
            section * peers + expert,
            (sections - 1 - section if crossing else section) * peers + (expert ^ distance),
        )
        for section in range(sections)
        for expert in range(peers)
    ]
    return lax.ppermute(block, ("section", "expert"), pairs)


def exchange(blocks, groups):
    return lax.all_to_all(
        blocks, ("section", "expert"), split_axis=0, concat_axis=0, axis_index_groups=groups, tiled=True
    )


def near_bundles(near_peers):
    return [(distance, 2) for distance in range(0, near_peers, 2)]


def splits(peers, capacity):
    return peers > 2 and peers & (peers - 1) == 0 and capacity % TILE_ROWS == 0


def per_device(grad_rows, owner_ids, saved_hidden, momentum):
    sections = lax.axis_size("section")
    peers = lax.axis_size("expert")
    slots = saved_hidden.shape[3]
    capacity = slots // peers
    count, width = grad_rows.shape[2:]
    ids = owner_ids[0].reshape(2, 1, count)
    shaped = lambda *shape: jax.ShapeDtypeStruct(shape, jnp.bfloat16)
    landing = lambda *shape: pltpu.VMEM(shape, jnp.bfloat16)
    last = (saved_hidden[0, 0, 0], momentum[0, 0])
    outs = (shaped(*momentum.shape[2:]),) * 2
    current = pltpu.VMEM(momentum.shape[2:], jnp.float32)
    split = splits(peers, capacity)
    groups = joint_groups(sections, peers, split)

    def hidden_over(hidden):
        return lax.ppermute(hidden, "section", [(i, sections - 1 - i) for i in range(sections)])

    if not split:
        packed = whole_call(
            functools.partial(pack_kernel, peers, capacity, sections),
            shaped(2, slots, width), (ids, grad_rows[0]),
        )
        arrived = exchange(packed.reshape(2 * peers, capacity, width), groups).reshape(2, slots, width)
        operands = (arrived, last[0], hidden_over(saved_hidden[0, 1, 0]), last[1])
        body = functools.partial(finish_kernel, sections)
        scratch = (current,)
    else:
        near_peers = peers // 2
        height = saved_hidden.shape[4]
        joint, *singles, near_hidden, turned = whole_call(
            functools.partial(pack_split_kernel, peers, capacity, sections),
            (shaped(2, near_peers * capacity, width),) + (landing(2 * capacity, width),) * (near_peers // 2)
            + tuple(landing(size * capacity, width) for _, size in near_bundles(near_peers))
            + (landing(height, slots),) * 2,
            (ids, grad_rows[0], saved_hidden.reshape(2, slots, height)),
            (
                pltpu.VMEM(ids.shape, jnp.int32),
                pltpu.VMEM(grad_rows.shape[1:], jnp.bfloat16),
                pltpu.VMEM((2, slots, height), jnp.bfloat16),
                pltpu.VMEM((2, near_peers * capacity, width), jnp.bfloat16),
                pltpu.SemaphoreType.DMA((5, 2)),
            ),
            in_spec=ANY,
            out_spec=(ANY,) + (VMEM,) * (near_peers // 2 + len(near_bundles(near_peers)) + 2),
        )
        pairs = near_peers // 2
        landed, relayed, mirrored = [], [], []
        for index, block in enumerate(singles[:pairs]):
            landed.append(direct(block, sections, peers, near_peers + 2 * index, False))
        for (distance, size), block in zip(near_bundles(near_peers), singles[pairs:]):
            block = direct(block, sections, peers, distance, True)
            mirrored.append(block)
            if size == 2:
                mirrored.append(direct(block[capacity:], sections, peers, 1, False))
        for block in landed:
            relayed.append(direct(block[capacity:], sections, peers, 1, False))
        far_hidden = hidden_over(turned)
        arrived = exchange(joint.reshape(peers, capacity, width), groups)
        operands = (arrived.reshape(joint.shape), *landed, *relayed, *mirrored, near_hidden, far_hidden, last[1])
        body = functools.partial(finish_split_kernel, peers, sections)
        scratch = (
            pltpu.VMEM(momentum.shape[2:], jnp.bfloat16),
            pltpu.VMEM(momentum.shape[2:], jnp.bfloat16),
            pltpu.SemaphoreType.DMA((2, pl.cdiv(width, min(WIDE, NARROW)))),
        )
    new_momentum, update_step = whole_call(
        body, outs, tuple(map(in_vmem, operands)), scratch,
        out_spec=ANY if split else VMEM,
    )
    return (new_momentum[None, None], update_step[None, None])


def solution(mesh):
    placed = (
        P("section", None, "expert", None),
        P("section", None, "expert", None),
        P("section", None, "expert", None, None),
        P("section", "expert", None, None),
    )

    return jax.shard_map(
        per_device,
        mesh=mesh,
        in_specs=placed,
        out_specs=(P("section", "expert", None, None), P("section", "expert", None, None)),
        check_vma=False,
    )
```
